32 devices in a mesh: frame: 4 (over y, x), tile: 8 (over z, core).
Axes of the slice: x: 2, y: 2, z: 4, core: 2. Of those that a mesh axis runs over, the one named last changes fastest.
Arguments:
- saved_codes: bfloat16 [8, 32, 32, 128], P('frame', 'tile'), may hold values from -1 to 1
- saved_scales: float32 [8, 32, 32], P('frame', 'tile'), may hold values from 0.5 to 2.5
- kernels: bfloat16 [2, 27, 128, 128], replicated, may hold values from -0.109375 to 0.109375
- norm_gains: float32 [2, 128], replicated, may hold values from 0.25 to 1.75
- cotangent: bfloat16 [8, 32, 32, 128], P('frame', 'tile'), may hold values from -13 to 13
Outputs:
- input_grad: bfloat16 [8, 32, 32, 128], P('frame', 'tile')
- kernel_grads: float32 [54, 128, 128], P(None, 'tile', 'frame')
The draws below stay inside these ranges and needn't reach their ends.
All inputs are finite; a program needn't handle non-finite values.
Results may differ from the reference program's by a relative error of at most 0.028.
Values may be sent and summed in bfloat16 or wider, within the bound.
A program may use at most 64 MiB of HBM per device.

```python
import math
import jax
import jax.numpy as jnp
from jax import lax

C = 128
LAYERS = 2
W = 32
NT = 8
NH = 32


def draw_cotangent(key, part):
    first = jax.random.fold_in(key, 0)
    frame_rise = 0.5 + 1.5 * jnp.arange(NT, dtype=jnp.float32) / NT
    row_rise = 0.6 + 1.2 * jnp.arange(NH, dtype=jnp.float32) / NH
    scale = frame_rise[:, None, None, None] * row_rise[None, :, None, None]
    base = jnp.clip(jax.random.normal(first, (NT, NH, W, C), jnp.float32), -3.5, 3.5)
    return (base * scale).astype(jnp.bfloat16)


def shard_levels(key, shape, pieces, least, high):
    factor_of, own = 1.0, jax.random.fold_in(key, 6)
    for position, shards_of in pieces:
        heights = jnp.exp(jax.random.uniform(jax.random.fold_in(own, position), (shards_of,), jnp.float32, least / len(pieces), high / len(pieces)))
        factor_of = factor_of * jnp.repeat(heights, shape[position] // shards_of).reshape([-1 if axis == position else 1 for axis in range(len(shape))])
    return factor_of


def noise(rng, shape, scale, reach, kind=jnp.bfloat16):
    return jnp.clip(scale * jax.random.normal(rng, shape, jnp.float32), -reach, reach).astype(kind)


def setup_inputs(seed: int = 0) -> dict:
    key_of = jax.random.split(jax.random.key(seed), 6)
    return {
        "saved_codes": jnp.clip(jax.random.uniform(key_of[0], (NT, NH, W, C), jnp.float32, -1.0, 1.0) * shard_levels(key_of[0], (NT, NH, W, C), ((0, 4), (1, 8)), -0.4, 0.0), -1.0, 1.0).astype(jnp.bfloat16),
        "saved_scales": jnp.clip(jnp.exp(math.log(2.5) - 1.609438 * jax.random.uniform(key_of[1], (NT, NH, W), jnp.float32) ** shard_levels(key_of[1], (NT, NH, W), ((0, 4), (1, 8)), -0.2, 0.2)), 0.5, 2.5),
        "kernels": noise(key_of[2], (LAYERS, 27, C, C), (27 * C) ** -0.5, 0.109375),
        "norm_gains": jnp.clip(1.0 + 0.15 * jax.random.normal(key_of[3], (LAYERS, C), jnp.float32), 0.25, 1.75),
        "cotangent": draw_cotangent(jax.random.fold_in(key_of[5], 71), 0),
    }


EPS = 1e-06

def convolve(inputs, weights):
    channels = weights.shape[-1]
    kernel = weights.reshape(3, 3, 3, channels, channels)
    result = lax.conv_general_dilated(inputs[None], kernel, (1, 1, 1), ((2, 0), (1, 1), (1, 1)), dimension_numbers=('NDHWC', 'DHWIO', 'NDHWC'), precision=lax.Precision.HIGHEST)
    return result[0]

def reference(saved_codes, saved_scales, kernels, norm_gains, cotangent):
    layer_in = (saved_codes.astype(jnp.float32) * saved_scales[..., None]).astype(jnp.bfloat16)
    inputs_list = []
    states = []
    for layer in range(LAYERS):
        inputs_list.append(layer_in)
        pre_norm = convolve(layer_in.astype(jnp.float32), kernels[layer].astype(jnp.float32))
        inverse = lax.rsqrt(lax.optimization_barrier(jnp.mean(pre_norm * pre_norm, axis=-1, keepdims=True)) + EPS)
        normed = pre_norm * inverse * norm_gains[layer]
        states.append((pre_norm, inverse, normed))
        layer_in = jax.nn.silu(normed).astype(jnp.bfloat16)
    upstream = cotangent
    grads_list = [None] * LAYERS
    for layer in reversed(range(LAYERS)):
        pre_norm, inverse, normed = states[layer]
        sigma = jax.nn.sigmoid(normed)
        scaled = norm_gains[layer] * upstream.astype(jnp.float32) * sigma * (1.0 + normed * (1.0 - sigma))
        mixed = lax.optimization_barrier(jnp.mean(pre_norm * scaled, axis=-1, keepdims=True))
        pre_grad = (inverse * scaled - pre_norm * inverse ** 3 * mixed).astype(jnp.bfloat16)
        pre_grad = lax.optimization_barrier(pre_grad).astype(jnp.float32)
        _, pullback = jax.vjp(convolve, inputs_list[layer].astype(jnp.float32), kernels[layer].astype(jnp.float32))
        input_part, kernel_part = pullback(pre_grad)
        grads_list[layer] = kernel_part
        upstream = input_part.astype(jnp.bfloat16)
    total_cells = NT * NH * W
    kernel_grads = jnp.stack(grads_list).reshape(LAYERS * 27, C, C) / jnp.sqrt(jnp.float32(total_cells))
    return (upstream, kernel_grads)
```

```python
import functools
import math

import jax
import jax.numpy as jnp
from jax import lax
from jax.experimental import pallas as pl
from jax.experimental.pallas import tpu as pltpu
from jax.sharding import PartitionSpec as P

EPS = 1e-06
MESH = pl.DeviceIdType.MESH
F32 = jnp.float32
BF16 = jnp.bfloat16


def sigmoid(value):
    return 1.0 / (1.0 + jnp.exp(-value))


def kernel(
    sizes,
    x_in,
    w_in,
    gains_ref,
    cot_in,
    grad_ref,
    kg_ref,
    ext,
    weights,
    turned,
    cot,
    patch,
    patch_back,
    z_keep,
    pair_out,
    pair_in,
    ring_out,
    ring_in,
    total,
    pack_out,
    pack_in,
    local_sem,
    halo_send,
    halo_recv,
    pair_send,
    pair_recv,
    ring_send,
    ring_recv,
    pack_send,
    pack_recv,
):
    nf, nt, layers, frames, rows, columns, channels = sizes
    f = lax.axis_index("frame")
    t = lax.axis_index("tile")
    pairs = nt // 2
    core = t % 2
    place = t // 2
    block = rows * columns
    cells = frames * block
    own_q = channels // nt
    own_o = channels // nf
    group = -(-27 // nf)

    x_copy = pltpu.make_async_copy(
        x_in, ext.at[0, frames : 2 * frames, 1 : 1 + rows], local_sem.at[0]
    )
    w_copies = [
        pltpu.make_async_copy(w_in.at[l], weights.at[l], local_sem.at[1 + l]) for l in range(layers)
    ]
    cot_copy = pltpu.make_async_copy(cot_in, cot, local_sem.at[1 + layers])
    for e in range(2 * layers):
        edge = jnp.zeros((2 * frames, 1, columns, channels), BF16)
        ext[e, :, 0:1] = edge
        ext[e, :, rows + 1 : rows + 2] = edge
        far = 0 if e < layers else frames
        ext[e, far : far + frames, 1 : 1 + rows] = jnp.zeros(
            (frames, rows, columns, channels), BF16
        )
    x_copy.start()
    for c in w_copies:
        c.start()
    cot_copy.start()

    offsets = {(0, 1), (0, nt - 1)}
    for df in (1, nf - 1):
        for dt in (0, 1, nt - 1):
            offsets.add((df, dt))
    for s in range(1, pairs):
        offsets.add((0, 2 * s))
    for s in range(1, nf):
        offsets.add((s, 0))
    offsets = sorted(offsets)
    barrier = pltpu.get_barrier_semaphore()
    for df, dt in offsets:
        pl.semaphore_signal(
            barrier,
            inc=1,
            device_id=((f + df) % nf, (t + dt) % nt),
            device_id_type=MESH,
        )
    pl.semaphore_wait(barrier, len(offsets))

    def halo(e):
        step = 1 if e < layers else -1
        own = frames if step > 0 else 0
        far = 0 if step > 0 else frames
        messages = []
        for index, (df, dt) in enumerate(((step, 0), (0, 1), (0, -1), (step, 1), (step, -1))):
            if dt == 0:
                src_rows, dst_rows = (1, 1 + rows), (1, 1 + rows)
            elif dt > 0:
                src_rows, dst_rows = (rows, rows + 1), (0, 1)
            else:
                src_rows, dst_rows = (1, 2), (rows + 1, rows + 2)
            start = far if df else own
            to_f, to_t, from_f, from_t = f + df, t + dt, f - df, t - dt
            can_send = (to_f >= 0) & (to_f < nf) & (to_t >= 0) & (to_t < nt)
            can_recv = (from_f >= 0) & (from_f < nf) & (from_t >= 0) & (from_t < nt)
            copy = pltpu.make_async_remote_copy(
                src_ref=ext.at[e, own : own + frames, src_rows[0] : src_rows[1]],
                dst_ref=ext.at[e, start : start + frames, dst_rows[0] : dst_rows[1]],
                send_sem=halo_send.at[e, index],
                recv_sem=halo_recv.at[e, index],
                device_id=((f + df) % nf, (t + dt) % nt),
                device_id_type=MESH,
            )
            messages.append((copy, can_send, can_recv))
        return messages

    halos = [halo(e) for e in range(2 * layers)]

    def send_halo(e):
        for copy, can_send, _ in halos[e]:
            pl.when(can_send)(copy.start)

    def wait_halo(e):
        for copy, _, can_recv in halos[e]:
            pl.when(can_recv)(copy.wait_recv)

    height = 2 * frames * (rows + 2) * columns
    column = lax.broadcasted_iota(jnp.int32, (height, channels), 0) % columns

    def fill(target, e):
        flat = ext[e].astype(F32).reshape(height, channels)
        before = jnp.where(column == 0, 0.0, pltpu.roll(flat, 1, 0)).astype(BF16)
        after = jnp.where(column == columns - 1, 0.0, pltpu.roll(flat, height - 1, 0)).astype(BF16)
        for c, value in enumerate((before, ext[e].reshape(height, channels), after)):
            value = value.reshape(2 * frames, rows + 2, columns, channels)
            for b in range(3):
                at = (3 * b + c) * channels
                target[:, at : at + channels] = value[:, b : b + rows].reshape(
                    2 * cells, channels
                )

    def turn(l):
        for k in range(27):
            a, m = k // 9, 8 - k % 9
            turned[l, a, m * channels : (m + 1) * channels, :] = weights[l, k].T

    def pair_copy(l, a):
        return pltpu.make_async_remote_copy(
            src_ref=pair_out.at[l, a, 1 - core],
            dst_ref=pair_in.at[l, a],
            send_sem=pair_send.at[l, a],
            recv_sem=pair_recv.at[l, a],
            device_id=(f, t + 1 - 2 * core),
            device_id_type=MESH,
        )

    def ring_copy(l, a, s):
        peer = (place + s) % pairs
        return pltpu.make_async_remote_copy(
            src_ref=ring_out.at[l, a, peer],
            dst_ref=ring_in.at[l, a, s - 1],
            send_sem=ring_send.at[l, a, s - 1],
            recv_sem=ring_recv.at[l, a, s - 1],
            device_id=(f, 2 * peer + core),
            device_id_type=MESH,
        )

    def pack_copy(l, s):
        peer = (f + s) % nf
        return pltpu.make_async_remote_copy(
            src_ref=pack_out.at[l, peer],
            dst_ref=pack_in.at[l, s - 1],
            send_sem=pack_send.at[l, s - 1],
            recv_sem=pack_recv.at[l, s - 1],
            device_id=(peer, t),
            device_id_type=MESH,
        )

    def kernel_terms(l, pre_grad):
        for a in range(3):
            part = lax.dot_general(
                patch[l, a * block : a * block + cells, :],
                pre_grad,
                (((0,), (0,)), ((), ())),
                preferred_element_type=F32,
            )
            part = part.astype(BF16).reshape(9, channels, channels)
            for d in range(nt):
                pair_out[l, a, d % 2, d // 2] = part[:, d * own_q : (d + 1) * own_q]
            pair_copy(l, a).start()

    def ring_stage(l):
        for a in range(3):
            pair_copy(l, a).wait_recv()
            for s in range(1, pairs):
                peer = (place + s) % pairs
                ring_out[l, a, peer] = (
                    pair_out[l, a, core, peer].astype(F32) + pair_in[l, a, peer].astype(F32)
                ).astype(BF16)
                ring_copy(l, a, s).start()
            total[l, 9 * a : 9 * a + 9] = pair_out[l, a, core, place].astype(F32) + pair_in[
                l, a, place
            ].astype(F32)

    lane_block = lax.broadcasted_iota(jnp.int32, (group, own_q, channels), 2) // own_o

    def pack_stage(l):
        for a in range(3):
            value = total[l, 9 * a : 9 * a + 9]
            for s in range(1, pairs):
                ring_copy(l, a, s).wait_recv()
                value = value + ring_in[l, a, s - 1].astype(F32)
            total[l, 9 * a : 9 * a + 9] = value
        for d in range(nf):
            packed = jnp.zeros((group, own_q, channels), F32)
            for j in range(nf):
                piece = total[l, j * group : (j + 1) * group]
                shift = ((j - d) * own_o) % channels
                if shift:
                    piece = pltpu.roll(
                        piece.reshape(group * own_q, channels), shift, 1
                    ).reshape(group, own_q, channels)
                packed = jnp.where(lane_block == j, piece, packed)
            pack_out[l, d] = packed.astype(BF16)
        for s in range(1, nf):
            pack_copy(l, s).start()

    def finish(l):
        value = pack_out[l, f].astype(F32)
        for s in range(1, nf):
            pack_copy(l, s).wait_recv()
            value = value + pack_in[l, s - 1].astype(F32)
        for j in range(nf):
            low, high = j * group, min(27, (j + 1) * group)
            if low >= high:
                break
            moved = value
            if j:
                moved = pltpu.roll(
                    value.reshape(group * own_q, channels), channels - j * own_o, 1
                ).reshape(group, own_q, channels)
            kg_ref[27 * l + low : 27 * l + high] = moved[: high - low, :, :own_o]

    x_copy.wait()
    send_halo(0)
    for l in range(layers):
        total[l, 27:] = jnp.zeros((nf * group - 27, own_q, channels), F32)
    for l in range(layers):
        w_copies[l].wait()
        if l == 0:
            turn(layers - 1 if layers == 1 else 0)
        else:
            turn(l)
        wait_halo(l)
        fill(patch.at[l], l)
        z = jnp.zeros((cells, channels), F32)
        for a in range(3):
            z = z + jnp.dot(
                patch[l, a * block : a * block + cells, :],
                weights[l, 9 * a : 9 * a + 9].reshape(9 * channels, channels),
                preferred_element_type=F32,
            )
        z_keep[l] = z
        if l + 1 < layers:
            inverse = lax.rsqrt(jnp.mean(z * z, axis=-1, keepdims=True) + EPS)
            normed = z * inverse * gains_ref[l : l + 1, :]
            ext[l + 1, frames : 2 * frames, 1 : 1 + rows] = (
                (normed * sigmoid(normed)).astype(BF16).reshape(frames, rows, columns, channels)
            )
            send_halo(l + 1)

    cot_copy.wait()
    upstream = cot[...].astype(F32).reshape(cells, channels)
    for l in reversed(range(layers)):
        e = layers + l
        z = z_keep[l]
        gain = gains_ref[l : l + 1, :]
        inverse = lax.rsqrt(jnp.mean(z * z, axis=-1, keepdims=True) + EPS)
        normed = z * inverse * gain
        sigma = sigmoid(normed)
        scaled = gain * upstream * sigma * (1.0 + normed * (1.0 - sigma))
        mixed = jnp.mean(z * scaled, axis=-1, keepdims=True)
        pre_grad = (inverse * scaled - z * (inverse * inverse * inverse * mixed)).astype(BF16)
        ext[e, 0:frames, 1 : 1 + rows] = pre_grad.reshape(frames, rows, columns, channels)
        send_halo(e)
        kernel_terms(l, pre_grad)
        if l + 1 < layers:
            pack_stage(l + 1)
        ring_stage(l)
        wait_halo(e)
        fill(patch_back, e)
        back = jnp.zeros((cells, channels), F32)
        for a in range(3):
            start = (2 - a) * block
            back = back + jnp.dot(
                patch_back[start : start + cells, :], turned[l, a], preferred_element_type=F32
            )
        back = back.astype(BF16)
        upstream = back.astype(F32)
        if l + 1 < layers:
            finish(l + 1)
    grad_ref[...] = back.reshape(frames, rows, columns, channels)
    pack_stage(0)
    finish(0)

    for e in range(2 * layers):
        for copy, can_send, _ in halos[e]:
            pl.when(can_send)(copy.wait_send)
    for l in range(layers):
        for a in range(3):
            pair_copy(l, a).wait_send()
            for s in range(1, pairs):
                ring_copy(l, a, s).wait_send()
        for s in range(1, nf):
            pack_copy(l, s).wait_send()


def local(saved_codes, saved_scales, kernels, norm_gains, cotangent):
    nf, nt = lax.axis_size("frame"), lax.axis_size("tile")
    frames, rows, columns, channels = saved_codes.shape
    layers = kernels.shape[0]
    assert frames == 2
    block = rows * columns
    cells = frames * block
    pairs = nt // 2
    own_q, own_o = channels // nt, channels // nf
    group = -(-27 // nf)
    layer_in = (saved_codes.astype(F32) * saved_scales[..., None]).astype(BF16)
    vmem = pl.BlockSpec(memory_space=pltpu.VMEM)
    anywhere = pl.BlockSpec(memory_space=pl.ANY)
    dma = pltpu.SemaphoreType.DMA
    input_grad, summed = pl.pallas_call(
        functools.partial(kernel, (nf, nt, layers, frames, rows, columns, channels)),
        out_shape=(
            jax.ShapeDtypeStruct((frames, rows, columns, channels), BF16),
            jax.ShapeDtypeStruct((27 * layers, own_q, own_o), F32),
        ),
        in_specs=[anywhere, anywhere, vmem, anywhere],
        out_specs=(vmem, vmem),
        scratch_shapes=[
            pltpu.VMEM((2 * layers, 2 * frames, rows + 2, columns, channels), BF16),
            pltpu.VMEM((layers, 27, channels, channels), BF16),
            pltpu.VMEM((layers, 3, 9 * channels, channels), BF16),
            pltpu.VMEM((frames, rows, columns, channels), BF16),
            pltpu.VMEM((layers, 2 * cells, 9 * channels), BF16),
            pltpu.VMEM((2 * cells, 9 * channels), BF16),
            pltpu.VMEM((layers, cells, channels), F32),
            pltpu.VMEM((layers, 3, 2, pairs, 9, own_q, channels), BF16),
            pltpu.VMEM((layers, 3, pairs, 9, own_q, channels), BF16),
            pltpu.VMEM((layers, 3, pairs, 9, own_q, channels), BF16),
            pltpu.VMEM((layers, 3, pairs - 1, 9, own_q, channels), BF16),
            pltpu.VMEM((layers, nf * group, own_q, channels), F32),
            pltpu.VMEM((layers, nf, group, own_q, channels), BF16),
            pltpu.VMEM((layers, nf - 1, group, own_q, channels), BF16),
            dma((2 + layers,)),
            dma((2 * layers, 5)),
            dma((2 * layers, 5)),
            dma((layers, 3)),
            dma((layers, 3)),
            dma((layers, 3, pairs - 1)),
            dma((layers, 3, pairs - 1)),
            dma((layers, nf - 1)),
            dma((layers, nf - 1)),
        ],
        compiler_params=pltpu.CompilerParams(
            collective_id=0, has_side_effects=True, vmem_limit_bytes=50 * 1024 * 1024
        ),
    )(layer_in, kernels, norm_gains, cotangent)
    total_cells = cells * nf * nt
    return input_grad, summed / jnp.float32(math.sqrt(total_cells))


def solution(mesh):
    in_specs = (
        P("frame", "tile", None, None),
        P("frame", "tile", None),
        P(),
        P(),
        P("frame", "tile", None, None),
    )
    out_specs = (P("frame", "tile", None, None), P(None, "tile", "frame"))
    return jax.shard_map(local, mesh=mesh, in_specs=in_specs, out_specs=out_specs, check_vma=False)
```

```python
import functools
import math

import jax
import jax.numpy as jnp
from jax import lax
from jax.experimental import pallas as pl
from jax.experimental.pallas import tpu as pltpu
from jax.sharding import PartitionSpec as P

EPS = 1e-06
MESH = pl.DeviceIdType.MESH
F32 = jnp.float32
BF16 = jnp.bfloat16


def sigmoid(value):
    return 1.0 / (1.0 + jnp.exp(-value))


def kernel(
    sizes,
    codes_in,
    scales_ref,
    w_in,
    gains_ref,
    cot_in,
    grad_ref,
    kg_ref,
    ext,
    weights,
    turned,
    cot,
    codes,
    patch,
    patch_back,
    z_keep,
    pair_out,
    pair_in,
    ring_out,
    ring_in,
    total,
    pack_out,
    pack_in,
    local_sem,
    halo_send,
    halo_recv,
    pair_send,
    pair_recv,
    ring_send,
    ring_recv,
    pack_send,
    pack_recv,
):
    nf, nt, layers, frames, rows, columns, channels = sizes
    f = lax.axis_index("frame")
    t = lax.axis_index("tile")
    pairs = nt // 2
    core = t % 2
    place = t // 2
    block = rows * columns
    cells = frames * block
    own_q = channels // nt
    own_o = channels // nf
    group = -(-27 // nf)

    x_copy = pltpu.make_async_copy(codes_in, codes, local_sem.at[0])
    w_copies = [
        pltpu.make_async_copy(w_in.at[l], weights.at[l], local_sem.at[1 + l]) for l in range(layers)
    ]
    cot_copy = pltpu.make_async_copy(cot_in, cot, local_sem.at[1 + layers])
    x_copy.start()
    for c in w_copies:
        c.start()
    cot_copy.start()
    for e in range(2 * layers):
        edge = jnp.zeros((2 * frames, 1, columns, channels), BF16)
        ext[e, :, 0:1] = edge
        ext[e, :, rows + 1 : rows + 2] = edge
        far = 0 if e < layers else frames
        ext[e, far : far + frames, 1 : 1 + rows] = jnp.zeros(
            (frames, rows, columns, channels), BF16
        )

    offsets = {(0, 1), (0, nt - 1)}
    for df in (1, nf - 1):
        for dt in (0, 1, nt - 1):
            offsets.add((df, dt))
    for s in range(1, pairs):
        offsets.add((0, 2 * s))
    for s in range(1, nf):
        offsets.add((s, 0))
    offsets = sorted(offsets)
    barrier = pltpu.get_barrier_semaphore()
    for df, dt in offsets:
        pl.semaphore_signal(
            barrier,
            inc=1,
            device_id=((f + df) % nf, (t + dt) % nt),
            device_id_type=MESH,
        )
    x_copy.wait()
    scales = scales_ref[...].reshape(frames * rows, columns).T
    for i in range(frames):
        for j in range(rows):
            at = i * rows + j
            ext[0, frames + i, 1 + j] = (codes[i, j].astype(F32) * scales[:, at : at + 1]).astype(
                BF16
            )
    pl.semaphore_wait(barrier, len(offsets))

    def halo(e):
        step = 1 if e < layers else -1
        own = frames if step > 0 else 0
        far = 0 if step > 0 else frames
        messages = []
        for index, (df, dt) in enumerate(((step, 0), (0, 1), (0, -1), (step, 1), (step, -1))):
            if dt == 0:
                src_rows, dst_rows = (1, 1 + rows), (1, 1 + rows)
            elif dt > 0:
                src_rows, dst_rows = (rows, rows + 1), (0, 1)
            else:
                src_rows, dst_rows = (1, 2), (rows + 1, rows + 2)
            start = far if df else own
            to_f, to_t, from_f, from_t = f + df, t + dt, f - df, t - dt
            can_send = (to_f >= 0) & (to_f < nf) & (to_t >= 0) & (to_t < nt)
            can_recv = (from_f >= 0) & (from_f < nf) & (from_t >= 0) & (from_t < nt)
            copy = pltpu.make_async_remote_copy(
                src_ref=ext.at[e, own : own + frames, src_rows[0] : src_rows[1]],
                dst_ref=ext.at[e, start : start + frames, dst_rows[0] : dst_rows[1]],
                send_sem=halo_send.at[e, index],
                recv_sem=halo_recv.at[e, index],
                device_id=((f + df) % nf, (t + dt) % nt),
                device_id_type=MESH,
            )
            messages.append((copy, can_send, can_recv))
        return messages

    halos = [halo(e) for e in range(2 * layers)]

    def send_halo(e):
        for copy, can_send, _ in halos[e]:
            pl.when(can_send)(copy.start)

    def wait_halo(e):
        for copy, _, can_recv in halos[e]:
            pl.when(can_recv)(copy.wait_recv)

    height = 2 * frames * (rows + 2) * columns
    column = lax.broadcasted_iota(jnp.int32, (height, channels), 0) % columns

    def fill(target, e):
        flat = ext[e].astype(F32).reshape(height, channels)
        before = jnp.where(column == 0, 0.0, pltpu.roll(flat, 1, 0)).astype(BF16)
        after = jnp.where(column == columns - 1, 0.0, pltpu.roll(flat, height - 1, 0)).astype(BF16)
        for c, value in enumerate((before, ext[e].reshape(height, channels), after)):
            value = value.reshape(2 * frames, rows + 2, columns, channels)
            for b in range(3):
                at = (3 * b + c) * channels
                target[:, at : at + channels] = value[:, b : b + rows].reshape(
                    2 * cells, channels
                )

    def turn(l):
        for k in range(27):
            a, m = k // 9, 8 - k % 9
            turned[l, a, m * channels : (m + 1) * channels, :] = weights[l, k].T

    def pair_copy(l, a):
        return pltpu.make_async_remote_copy(
            src_ref=pair_out.at[l, a, 1 - core],
            dst_ref=pair_in.at[l, a],
            send_sem=pair_send.at[l, a],
            recv_sem=pair_recv.at[l, a],
            device_id=(f, t + 1 - 2 * core),
            device_id_type=MESH,
        )

    def ring_copy(l, a, s):
        peer = (place + s) % pairs
        return pltpu.make_async_remote_copy(
            src_ref=ring_out.at[l, a, peer],
            dst_ref=ring_in.at[l, a, s - 1],
            send_sem=ring_send.at[l, a, s - 1],
            recv_sem=ring_recv.at[l, a, s - 1],
            device_id=(f, 2 * peer + core),
            device_id_type=MESH,
        )

    def pack_copy(l, s):
        peer = (f + s) % nf
        return pltpu.make_async_remote_copy(
            src_ref=pack_out.at[l, peer],
            dst_ref=pack_in.at[l, s - 1],
            send_sem=pack_send.at[l, s - 1],
            recv_sem=pack_recv.at[l, s - 1],
            device_id=(peer, t),
            device_id_type=MESH,
        )

    def kernel_terms(l, pre_grad):
        for a in range(3):
            part = lax.dot_general(
                patch[l, a * block : a * block + cells, :],
                pre_grad,
                (((0,), (0,)), ((), ())),
                preferred_element_type=F32,
            )
            part = part.astype(BF16).reshape(9, channels, channels)
            for d in range(nt):
                pair_out[l, a, d % 2, d // 2] = part[:, d * own_q : (d + 1) * own_q]
            pair_copy(l, a).start()

    def ring_stage(l):
        for a in range(3):
            pair_copy(l, a).wait_recv()
            for s in range(1, pairs):
                peer = (place + s) % pairs
                ring_out[l, a, peer] = (
                    pair_out[l, a, core, peer].astype(F32) + pair_in[l, a, peer].astype(F32)
                ).astype(BF16)
                ring_copy(l, a, s).start()
            total[l, 9 * a : 9 * a + 9] = pair_out[l, a, core, place].astype(F32) + pair_in[
                l, a, place
            ].astype(F32)

    lane_block = lax.broadcasted_iota(jnp.int32, (group, own_q, channels), 2) // own_o

    def pack_stage(l):
        for a in range(3):
            value = total[l, 9 * a : 9 * a + 9]
            for s in range(1, pairs):
                ring_copy(l, a, s).wait_recv()
                value = value + ring_in[l, a, s - 1].astype(F32)
            total[l, 9 * a : 9 * a + 9] = value
        for d in range(nf):
            packed = jnp.zeros((group, own_q, channels), F32)
            for j in range(nf):
                piece = total[l, j * group : (j + 1) * group]
                shift = ((j - d) * own_o) % channels
                if shift:
                    piece = pltpu.roll(
                        piece.reshape(group * own_q, channels), shift, 1
                    ).reshape(group, own_q, channels)
                packed = jnp.where(lane_block == j, piece, packed)
            pack_out[l, d] = packed.astype(BF16)
        for s in range(1, nf):
            pack_copy(l, s).start()

    def finish(l):
        value = pack_out[l, f].astype(F32)
        for s in range(1, nf):
            pack_copy(l, s).wait_recv()
            value = value + pack_in[l, s - 1].astype(F32)
        for j in range(nf):
            low, high = j * group, min(27, (j + 1) * group)
            if low >= high:
                break
            moved = value
            if j:
                moved = pltpu.roll(
                    value.reshape(group * own_q, channels), channels - j * own_o, 1
                ).reshape(group, own_q, channels)
            kg_ref[27 * l + low : 27 * l + high] = moved[: high - low, :, :own_o]

    send_halo(0)
    for l in range(layers):
        total[l, 27:] = jnp.zeros((nf * group - 27, own_q, channels), F32)
    for l in range(layers):
        w_copies[l].wait()
        if l == 0:
            turn(layers - 1 if layers == 1 else 0)
        else:
            turn(l)
        wait_halo(l)
        fill(patch.at[l], l)
        z = jnp.zeros((cells, channels), F32)
        for a in range(3):
            z = z + jnp.dot(
                patch[l, a * block : a * block + cells, :],
                weights[l, 9 * a : 9 * a + 9].reshape(9 * channels, channels),
                preferred_element_type=F32,
            )
        z_keep[l] = z
        if l + 1 < layers:
            inverse = lax.rsqrt(jnp.mean(z * z, axis=-1, keepdims=True) + EPS)
            normed = z * inverse * gains_ref[l : l + 1, :]
            ext[l + 1, frames : 2 * frames, 1 : 1 + rows] = (
                (normed * sigmoid(normed)).astype(BF16).reshape(frames, rows, columns, channels)
            )
            send_halo(l + 1)

    cot_copy.wait()
    upstream = cot[...].astype(F32).reshape(cells, channels)
    for l in reversed(range(layers)):
        e = layers + l
        z = z_keep[l]
        gain = gains_ref[l : l + 1, :]
        inverse = lax.rsqrt(jnp.mean(z * z, axis=-1, keepdims=True) + EPS)
        normed = z * inverse * gain
        sigma = sigmoid(normed)
        scaled = gain * upstream * sigma * (1.0 + normed * (1.0 - sigma))
        mixed = jnp.mean(z * scaled, axis=-1, keepdims=True)
        pre_grad = (inverse * scaled - z * (inverse * inverse * inverse * mixed)).astype(BF16)
        ext[e, 0:frames, 1 : 1 + rows] = pre_grad.reshape(frames, rows, columns, channels)
        send_halo(e)
        kernel_terms(l, pre_grad)
        ring_stage(l)
        if l + 1 < layers:
            pack_stage(l + 1)
        wait_halo(e)
        fill(patch_back, e)
        back = jnp.zeros((cells, channels), F32)
        for a in range(3):
            start = (2 - a) * block
            back = back + jnp.dot(
                patch_back[start : start + cells, :], turned[l, a], preferred_element_type=F32
            )
        back = back.astype(BF16)
        upstream = back.astype(F32)
        if l + 1 < layers:
            finish(l + 1)
    grad_ref[...] = back.reshape(frames, rows, columns, channels)
    pack_stage(0)
    finish(0)

    for e in range(2 * layers):
        for copy, can_send, _ in halos[e]:
            pl.when(can_send)(copy.wait_send)
    for l in range(layers):
        for a in range(3):
            pair_copy(l, a).wait_send()
            for s in range(1, pairs):
                ring_copy(l, a, s).wait_send()
        for s in range(1, nf):
            pack_copy(l, s).wait_send()


def local(saved_codes, saved_scales, kernels, norm_gains, cotangent):
    nf, nt = lax.axis_size("frame"), lax.axis_size("tile")
    frames, rows, columns, channels = saved_codes.shape
    layers = kernels.shape[0]
    assert frames == 2
    block = rows * columns
    cells = frames * block
    pairs = nt // 2
    own_q, own_o = channels // nt, channels // nf
    group = -(-27 // nf)
    vmem = pl.BlockSpec(memory_space=pltpu.VMEM)
    hbm = pl.BlockSpec(memory_space=pltpu.HBM)
    dma = pltpu.SemaphoreType.DMA
    input_grad, summed = pl.pallas_call(
        functools.partial(kernel, (nf, nt, layers, frames, rows, columns, channels)),
        out_shape=(
            jax.ShapeDtypeStruct((frames, rows, columns, channels), BF16),
            jax.ShapeDtypeStruct((27 * layers, own_q, own_o), F32),
        ),
        in_specs=[hbm, vmem, hbm, vmem, hbm],
        out_specs=(vmem, vmem),
        scratch_shapes=[
            pltpu.VMEM((2 * layers, 2 * frames, rows + 2, columns, channels), BF16),
            pltpu.VMEM((layers, 27, channels, channels), BF16),
            pltpu.VMEM((layers, 3, 9 * channels, channels), BF16),
            pltpu.VMEM((frames, rows, columns, channels), BF16),
            pltpu.VMEM((frames, rows, columns, channels), BF16),
            pltpu.VMEM((layers, 2 * cells, 9 * channels), BF16),
            pltpu.VMEM((2 * cells, 9 * channels), BF16),
            pltpu.VMEM((layers, cells, channels), F32),
            pltpu.VMEM((layers, 3, 2, pairs, 9, own_q, channels), BF16),
            pltpu.VMEM((layers, 3, pairs, 9, own_q, channels), BF16),
            pltpu.VMEM((layers, 3, pairs, 9, own_q, channels), BF16),
            pltpu.VMEM((layers, 3, pairs - 1, 9, own_q, channels), BF16),
            pltpu.VMEM((layers, nf * group, own_q, channels), F32),
            pltpu.VMEM((layers, nf, group, own_q, channels), BF16),
            pltpu.VMEM((layers, nf - 1, group, own_q, channels), BF16),
            dma((2 + layers,)),
            dma((2 * layers, 5)),
            dma((2 * layers, 5)),
            dma((layers, 3)),
            dma((layers, 3)),
            dma((layers, 3, pairs - 1)),
            dma((layers, 3, pairs - 1)),
            dma((layers, nf - 1)),
            dma((layers, nf - 1)),
        ],
        compiler_params=pltpu.CompilerParams(
            collective_id=0, has_side_effects=True, vmem_limit_bytes=66_500_000
        ),
    )(saved_codes, saved_scales, kernels, norm_gains, cotangent)
    total_cells = cells * nf * nt
    return input_grad, summed / jnp.float32(math.sqrt(total_cells))


def solution(mesh):
    in_specs = (
        P("frame", "tile", None, None),
        P("frame", "tile", None),
        P(),
        P(),
        P("frame", "tile", None, None),
    )
    out_specs = (P("frame", "tile", None, None), P(None, "tile", "frame"))
    return jax.shard_map(local, mesh=mesh, in_specs=in_specs, out_specs=out_specs, check_vma=False)
```

```python
import functools
import math

import jax
import jax.numpy as jnp
from jax import lax
from jax.experimental import pallas as pl
from jax.experimental.pallas import tpu as pltpu
from jax.sharding import PartitionSpec as P

EPS = 1e-06
MESH = pl.DeviceIdType.MESH
F32 = jnp.float32
BF16 = jnp.bfloat16


def sigmoid(value):
    return 1.0 / (1.0 + jnp.exp(-value))


def kernel(
    sizes,
    codes_in,
    scales_ref,
    w_in,
    gains_ref,
    cot_in,
    grad_ref,
    kg_ref,
    ext,
    weights,
    turned,
    cot,
    codes,
    patch,
    patch_back,
    z_keep,
    terms,
    pair_out,
    pair_in,
    ring_out,
    ring_in,
    total,
    pack_out,
    pack_in,
    wide_pair_out,
    wide_pair_in,
    wide_frame_out,
    wide_frame_in,
    wide_total,
    wide_ring_out,
    wide_ring_in,
    local_sem,
    halo_send,
    halo_recv,
    pair_send,
    pair_recv,
    ring_send,
    ring_recv,
    pack_send,
    pack_recv,
    wide_pair_send,
    wide_pair_recv,
    wide_frame_send,
    wide_frame_recv,
    wide_ring_send,
    wide_ring_recv,
):
    nf, nt, layers, frames, rows, columns, channels = sizes
    f = lax.axis_index("frame")
    t = lax.axis_index("tile")
    pairs = nt // 2
    core = t % 2
    place = t // 2
    block = rows * columns
    cells = frames * block
    own_q = channels // nt
    own_o = channels // nf
    group, wide = -(-9 // nf), -(-18 // nf)

    x_copy = pltpu.make_async_copy(codes_in, codes, local_sem.at[0])
    w_copies = [
        pltpu.make_async_copy(w_in.at[l], weights.at[l], local_sem.at[1 + l]) for l in range(layers)
    ]
    cot_copy = pltpu.make_async_copy(cot_in, cot, local_sem.at[1 + layers])
    x_copy.start()
    for c in w_copies:
        c.start()
    cot_copy.start()
    for e in range(2 * layers):
        edge = jnp.zeros((2 * frames, 1, columns, channels), BF16)
        ext[e, :, 0:1] = edge
        ext[e, :, rows + 1 : rows + 2] = edge
        far = 0 if e < layers else frames
        ext[e, far : far + frames, 1 : 1 + rows] = jnp.zeros(
            (frames, rows, columns, channels), BF16
        )

    offsets = {(0, 1), (0, nt - 1)}
    for df in (1, nf - 1):
        for dt in (0, 1, nt - 1):
            offsets.add((df, dt))
    for s in range(1, pairs):
        offsets.add((0, 2 * s))
    for s in range(1, nf):
        offsets.add((s, 0))
    offsets = sorted(offsets)
    barrier = pltpu.get_barrier_semaphore()
    for df, dt in offsets:
        pl.semaphore_signal(
            barrier,
            inc=1,
            device_id=((f + df) % nf, (t + dt) % nt),
            device_id_type=MESH,
        )
    x_copy.wait()
    scales = scales_ref[...].reshape(frames * rows, columns).T
    for i in range(frames):
        for j in range(rows):
            at = i * rows + j
            ext[0, frames + i, 1 + j] = (codes[i, j].astype(F32) * scales[:, at : at + 1]).astype(
                BF16
            )
    pl.semaphore_wait(barrier, len(offsets))

    def halo(e):
        step = 1 if e < layers else -1
        own = frames if step > 0 else 0
        far = 0 if step > 0 else frames
        messages = []
        for index, (df, dt) in enumerate(((step, 0), (0, 1), (0, -1), (step, 1), (step, -1))):
            if dt == 0:
                src_rows, dst_rows = (1, 1 + rows), (1, 1 + rows)
            elif dt > 0:
                src_rows, dst_rows = (rows, rows + 1), (0, 1)
            else:
                src_rows, dst_rows = (1, 2), (rows + 1, rows + 2)
            start = far if df else own
            to_f, to_t, from_f, from_t = f + df, t + dt, f - df, t - dt
            can_send = (to_f >= 0) & (to_f < nf) & (to_t >= 0) & (to_t < nt)
            can_recv = (from_f >= 0) & (from_f < nf) & (from_t >= 0) & (from_t < nt)
            copy = pltpu.make_async_remote_copy(
                src_ref=ext.at[e, own : own + frames, src_rows[0] : src_rows[1]],
                dst_ref=ext.at[e, start : start + frames, dst_rows[0] : dst_rows[1]],
                send_sem=halo_send.at[e, index],
                recv_sem=halo_recv.at[e, index],
                device_id=((f + df) % nf, (t + dt) % nt),
                device_id_type=MESH,
            )
            messages.append((copy, can_send, can_recv))
        return messages

    halos = [halo(e) for e in range(2 * layers)]

    def send_halo(e):
        for copy, can_send, _ in halos[e]:
            pl.when(can_send)(copy.start)

    def wait_halo(e):
        for copy, _, can_recv in halos[e]:
            pl.when(can_recv)(copy.wait_recv)

    height = 2 * frames * (rows + 2) * columns
    column = lax.broadcasted_iota(jnp.int32, (height, channels), 0) % columns

    def fill(target, e):
        flat = ext[e].astype(F32).reshape(height, channels)
        before = jnp.where(column == 0, 0.0, pltpu.roll(flat, 1, 0)).astype(BF16)
        after = jnp.where(column == columns - 1, 0.0, pltpu.roll(flat, height - 1, 0)).astype(BF16)
        for c, value in enumerate((before, ext[e].reshape(height, channels), after)):
            value = value.reshape(2 * frames, rows + 2, columns, channels)
            for b in range(3):
                at = (3 * b + c) * channels
                target[:, at : at + channels] = value[:, b : b + rows].reshape(
                    2 * cells, channels
                )

    def turn(l):
        for k in range(27):
            a, m = k // 9, 8 - k % 9
            turned[l, a, m * channels : (m + 1) * channels, :] = weights[l, k].T

    def remote(source, target, sends, recvs, device):
        return pltpu.make_async_remote_copy(
            src_ref=source,
            dst_ref=target,
            send_sem=sends,
            recv_sem=recvs,
            device_id=device,
            device_id_type=MESH,
        )

    partner = (f, t + 1 - 2 * core)

    def pair_copy(l):
        return remote(
            pair_out.at[l, 1 - core], pair_in.at[l], pair_send.at[l], pair_recv.at[l], partner
        )

    def ring_copy(l, s):
        peer = (place + s) % pairs
        return remote(
            ring_out.at[l, peer],
            ring_in.at[l, s - 1],
            ring_send.at[l, s - 1],
            ring_recv.at[l, s - 1],
            (f, 2 * peer + core),
        )

    def pack_copy(l, s):
        peer = (f + s) % nf
        return remote(
            pack_out.at[l, peer],
            pack_in.at[l, s - 1],
            pack_send.at[l, s - 1],
            pack_recv.at[l, s - 1],
            (peer, t),
        )

    def wide_pair_copy(l, d):
        return remote(
            wide_pair_out.at[l, d, 1 - core],
            wide_pair_in.at[l, d],
            wide_pair_send.at[l, d],
            wide_pair_recv.at[l, d],
            partner,
        )

    def wide_frame_copy(l, s):
        peer = (f + s) % nf
        return remote(
            wide_frame_out.at[l, peer],
            wide_frame_in.at[l, s - 1],
            wide_frame_send.at[l, s - 1],
            wide_frame_recv.at[l, s - 1],
            (peer, t),
        )

    def wide_ring_copy(l, s):
        peer = (place + s) % pairs
        return remote(
            wide_ring_out.at[l, peer],
            wide_ring_in.at[l, s - 1],
            wide_ring_send.at[l, s - 1],
            wide_ring_recv.at[l, s - 1],
            (f, 2 * peer + core),
        )

    def packed(source, size, d):
        height = source.shape[1]
        lane_block = lax.broadcasted_iota(jnp.int32, (size * height, channels), 1) // own_o
        result = jnp.zeros((size * height, channels), F32)
        for j in range(nf):
            piece = source[j * size : (j + 1) * size].reshape(size * height, channels)
            shift = ((j - d) * own_o) % channels
            if shift:
                piece = pltpu.roll(piece, shift, 1)
            result = jnp.where(lane_block == j, piece, result)
        return result.reshape(size, height, channels)

    def unpack(value, size, first, count):
        for j in range(nf):
            low, high = j * size, min(count, (j + 1) * size)
            if low >= high:
                break
            moved = value
            if j:
                moved = pltpu.roll(
                    value.reshape(size * own_q, channels), channels - j * own_o, 1
                ).reshape(size, own_q, channels)
            kg_ref[first + low : first + high] = moved[: high - low, :, :own_o]

    def kernel_term(l, a, pre_grad):
        part = lax.dot_general(
            patch[l, a * block : a * block + cells, :],
            pre_grad,
            (((0,), (0,)), ((), ())),
            preferred_element_type=F32,
        )
        return part.reshape(9, channels, channels)

    def kernel_terms(l, pre_grad):
        for a in (1, 2):
            terms[9 * a - 9 : 9 * a] = kernel_term(l, a, pre_grad)
        for d in range(nf):
            part = packed(terms, wide, d).astype(BF16)
            for q in range(nt):
                wide_pair_out[l, d, q % 2, q // 2] = part[:, q * own_q : (q + 1) * own_q]
            wide_pair_copy(l, d).start()
        part = kernel_term(l, 0, pre_grad).astype(BF16)
        for q in range(nt):
            pair_out[l, q % 2, q // 2] = part[:, q * own_q : (q + 1) * own_q]
        pair_copy(l).start()

    def ring_stage(l):
        for s in range(1, nf):
            peer = (f + s) % nf
            wide_pair_copy(l, peer).wait_recv()
            wide_frame_out[l, peer] = (
                wide_pair_out[l, peer, core].astype(F32) + wide_pair_in[l, peer].astype(F32)
            ).astype(BF16)
            wide_frame_copy(l, s).start()
        pair_copy(l).wait_recv()
        for s in range(1, pairs):
            peer = (place + s) % pairs
            ring_out[l, peer] = (
                pair_out[l, core, peer].astype(F32) + pair_in[l, peer].astype(F32)
            ).astype(BF16)
            ring_copy(l, s).start()
        total[l, 0:9] = pair_out[l, core, place].astype(F32) + pair_in[l, place].astype(F32)
        wide_pair_copy(l, f).wait_recv()
        wide_total[l] = wide_pair_out[l, f, core].astype(F32) + wide_pair_in[l, f].astype(F32)

    def pack_stage(l):
        for s in range(1, nf):
            wide_frame_copy(l, s).wait_recv()

        def wide_sum(p):
            value = wide_total[l, p]
            for s in range(1, nf):
                value = value + wide_frame_in[l, s - 1, p].astype(F32)
            return value

        for s in range(1, pairs):
            peer = (place + s) % pairs
            wide_ring_out[l, peer] = wide_sum(peer).astype(BF16)
            wide_ring_copy(l, s).start()
        wide_total[l, place] = wide_sum(place)
        value = total[l, 0:9]
        for s in range(1, pairs):
            ring_copy(l, s).wait_recv()
            value = value + ring_in[l, s - 1].astype(F32)
        total[l, 0:9] = value
        for d in range(nf):
            pack_out[l, d] = packed(total.at[l], group, d).astype(BF16)
        for s in range(1, nf):
            pack_copy(l, s).start()

    def finish(l):
        value = wide_total[l, place]
        for s in range(1, pairs):
            wide_ring_copy(l, s).wait_recv()
            value = value + wide_ring_in[l, s - 1].astype(F32)
        unpack(value * scale, wide, 27 * l + 9, 18)
        value = pack_out[l, f].astype(F32)
        for s in range(1, nf):
            pack_copy(l, s).wait_recv()
            value = value + pack_in[l, s - 1].astype(F32)
        unpack(value * scale, group, 27 * l, 9)

    scale = 1.0 / math.sqrt(cells * nf * nt)
    send_halo(0)
    for l in range(layers):
        if nf * group > 9:
            total[l, 9:] = jnp.zeros((nf * group - 9, own_q, channels), F32)
    if nf * wide > 18:
        terms[18:] = jnp.zeros((nf * wide - 18, channels, channels), F32)
    for l in range(layers):
        w_copies[l].wait()
        if l == 0:
            turn(layers - 1 if layers == 1 else 0)
        else:
            turn(l)
        wait_halo(l)
        fill(patch.at[l], l)
        z = jnp.zeros((cells, channels), F32)
        for a in range(3):
            z = z + jnp.dot(
                patch[l, a * block : a * block + cells, :],
                weights[l, 9 * a : 9 * a + 9].reshape(9 * channels, channels),
                preferred_element_type=F32,
            )
        z_keep[l] = z
        if l + 1 < layers:
            inverse = lax.rsqrt(jnp.mean(z * z, axis=-1, keepdims=True) + EPS)
            normed = z * inverse * gains_ref[l : l + 1, :]
            ext[l + 1, frames : 2 * frames, 1 : 1 + rows] = (
                (normed * sigmoid(normed)).astype(BF16).reshape(frames, rows, columns, channels)
            )
            send_halo(l + 1)

    cot_copy.wait()
    upstream = cot[...].astype(F32).reshape(cells, channels)
    for l in reversed(range(layers)):
        e = layers + l
        z = z_keep[l]
        gain = gains_ref[l : l + 1, :]
        inverse = lax.rsqrt(jnp.mean(z * z, axis=-1, keepdims=True) + EPS)
        normed = z * inverse * gain
        sigma = sigmoid(normed)
        scaled = gain * upstream * sigma * (1.0 + normed * (1.0 - sigma))
        mixed = jnp.mean(z * scaled, axis=-1, keepdims=True)
        pre_grad = (inverse * scaled - z * (inverse * inverse * inverse * mixed)).astype(BF16)
        ext[e, 0:frames, 1 : 1 + rows] = pre_grad.reshape(frames, rows, columns, channels)
        send_halo(e)
        kernel_terms(l, pre_grad)
        ring_stage(l)
        if l + 1 < layers:
            pack_stage(l + 1)
        wait_halo(e)
        fill(patch_back, e)
        back = jnp.zeros((cells, channels), F32)
        for a in range(3):
            start = (2 - a) * block
            back = back + jnp.dot(
                patch_back[start : start + cells, :], turned[l, a], preferred_element_type=F32
            )
        back = back.astype(BF16)
        upstream = back.astype(F32)
        if l + 1 < layers:
            finish(l + 1)
    grad_ref[...] = back.reshape(frames, rows, columns, channels)
    pack_stage(0)
    finish(0)

    for e in range(2 * layers):
        for copy, can_send, _ in halos[e]:
            pl.when(can_send)(copy.wait_send)
    for l in range(layers):
        pair_copy(l).wait_send()
        for d in range(nf):
            wide_pair_copy(l, d).wait_send()
        for s in range(1, pairs):
            ring_copy(l, s).wait_send()
            wide_ring_copy(l, s).wait_send()
        for s in range(1, nf):
            pack_copy(l, s).wait_send()
            wide_frame_copy(l, s).wait_send()


def local(saved_codes, saved_scales, kernels, norm_gains, cotangent):
    nf, nt = lax.axis_size("frame"), lax.axis_size("tile")
    frames, rows, columns, channels = saved_codes.shape
    layers = kernels.shape[0]
    assert frames == 2
    block = rows * columns
    cells = frames * block
    pairs = nt // 2
    own_q, own_o = channels // nt, channels // nf
    group, wide = -(-9 // nf), -(-18 // nf)
    vmem = pl.BlockSpec(memory_space=pltpu.VMEM)
    hbm = pl.BlockSpec(memory_space=pltpu.HBM)
    dma = pltpu.SemaphoreType.DMA
    input_grad, summed = pl.pallas_call(
        functools.partial(kernel, (nf, nt, layers, frames, rows, columns, channels)),
        out_shape=(
            jax.ShapeDtypeStruct((frames, rows, columns, channels), BF16),
            jax.ShapeDtypeStruct((27 * layers, own_q, own_o), F32),
        ),
        in_specs=[hbm, vmem, hbm, vmem, hbm],
        out_specs=(vmem, vmem),
        scratch_shapes=[
            pltpu.VMEM((2 * layers, 2 * frames, rows + 2, columns, channels), BF16),
            pltpu.VMEM((layers, 27, channels, channels), BF16),
            pltpu.VMEM((layers, 3, 9 * channels, channels), BF16),
            pltpu.VMEM((frames, rows, columns, channels), BF16),
            pltpu.VMEM((frames, rows, columns, channels), BF16),
            pltpu.VMEM((layers, 2 * cells, 9 * channels), BF16),
            pltpu.VMEM((2 * cells, 9 * channels), BF16),
            pltpu.VMEM((layers, cells, channels), F32),
            pltpu.VMEM((nf * wide, channels, channels), F32),
            pltpu.VMEM((layers, 2, pairs, 9, own_q, channels), BF16),
            pltpu.VMEM((layers, pairs, 9, own_q, channels), BF16),
            pltpu.VMEM((layers, pairs, 9, own_q, channels), BF16),
            pltpu.VMEM((layers, pairs - 1, 9, own_q, channels), BF16),
            pltpu.VMEM((layers, nf * group, own_q, channels), F32),
            pltpu.VMEM((layers, nf, group, own_q, channels), BF16),
            pltpu.VMEM((layers, nf - 1, group, own_q, channels), BF16),
            pltpu.VMEM((layers, nf, 2, pairs, wide, own_q, channels), BF16),
            pltpu.VMEM((layers, nf, pairs, wide, own_q, channels), BF16),
            pltpu.VMEM((layers, nf, pairs, wide, own_q, channels), BF16),
            pltpu.VMEM((layers, nf - 1, pairs, wide, own_q, channels), BF16),
            pltpu.VMEM((layers, pairs, wide, own_q, channels), F32),
            pltpu.VMEM((layers, pairs, wide, own_q, channels), BF16),
            pltpu.VMEM((layers, pairs - 1, wide, own_q, channels), BF16),
            dma((2 + layers,)),
            dma((2 * layers, 5)),
            dma((2 * layers, 5)),
            dma((layers,)),
            dma((layers,)),
            dma((layers, pairs - 1)),
            dma((layers, pairs - 1)),
            dma((layers, nf - 1)),
            dma((layers, nf - 1)),
            dma((layers, nf)),
            dma((layers, nf)),
            dma((layers, nf - 1)),
            dma((layers, nf - 1)),
            dma((layers, pairs - 1)),
            dma((layers, pairs - 1)),
        ],
        compiler_params=pltpu.CompilerParams(
            collective_id=0, has_side_effects=True, vmem_limit_bytes=65_700_000
        ),
    )(saved_codes, saved_scales, kernels, norm_gains, cotangent)
    return input_grad, summed


def solution(mesh):
    in_specs = (
        P("frame", "tile", None, None),
        P("frame", "tile", None),
        P(),
        P(),
        P("frame", "tile", None, None),
    )
    out_specs = (P("frame", "tile", None, None), P(None, "tile", "frame"))
    return jax.shard_map(local, mesh=mesh, in_specs=in_specs, out_specs=out_specs, check_vma=False)
```

```python
import functools
import math

import jax
import jax.numpy as jnp
from jax import lax
from jax.experimental import pallas as pl
from jax.experimental.pallas import tpu as pltpu
from jax.sharding import PartitionSpec as P

EPS = 1e-06
MESH = pl.DeviceIdType.MESH
F32 = jnp.float32
BF16 = jnp.bfloat16


def sigmoid(value):
    return 1.0 / (1.0 + jnp.exp(-value))


def kernel(
    sizes,
    codes_in,
    scales_ref,
    w_in,
    gains_ref,
    cot_in,
    grad_ref,
    kg_ref,
    ext,
    weights,
    turned,
    cot,
    codes,
    patch,
    patch_back,
    z_keep,
    summed,
    terms,
    pair_out,
    pair_in,
    ring_out,
    ring_in,
    total,
    pack_out,
    pack_in,
    wide_pair_out,
    wide_pair_in,
    wide_frame_out,
    wide_frame_in,
    wide_total,
    wide_ring_out,
    wide_ring_in,
    local_sem,
    halo_send,
    halo_recv,
    pair_send,
    pair_recv,
    ring_send,
    ring_recv,
    pack_send,
    pack_recv,
    wide_pair_send,
    wide_pair_recv,
    wide_frame_send,
    wide_frame_recv,
    wide_ring_send,
    wide_ring_recv,
):
    nf, nt, layers, frames, rows, columns, channels = sizes
    f = lax.axis_index("frame")
    t = lax.axis_index("tile")
    pairs = nt // 2
    core = t % 2
    place = t // 2
    block = rows * columns
    cells = frames * block
    own_q = channels // nt
    own_o = channels // nf
    group, wide = -(-9 // nf), -(-18 // nf)

    x_copy = pltpu.make_async_copy(codes_in, codes, local_sem.at[0])
    w_copies = [
        pltpu.make_async_copy(w_in.at[l], weights.at[l], local_sem.at[1 + l]) for l in range(layers)
    ]
    cot_copy = pltpu.make_async_copy(cot_in, cot, local_sem.at[1 + layers])
    x_copy.start()
    for c in w_copies:
        c.start()
    cot_copy.start()
    for e in range(2 * layers):
        edge = jnp.zeros((2 * frames, 1, columns, channels), BF16)
        ext[e, :, 0:1] = edge
        ext[e, :, rows + 1 : rows + 2] = edge
        far = 0 if e < layers else frames
        ext[e, far : far + frames, 1 : 1 + rows] = jnp.zeros(
            (frames, rows, columns, channels), BF16
        )

    offsets = {(0, 1), (0, nt - 1)}
    for df in (1, nf - 1):
        for dt in (0, 1, nt - 1):
            offsets.add((df, dt))
    for s in range(1, pairs):
        offsets.add((0, 2 * s))
    for s in range(1, nf):
        offsets.add((s, 0))
    offsets = sorted(offsets)
    barrier = pltpu.get_barrier_semaphore()
    for df, dt in offsets:
        pl.semaphore_signal(
            barrier,
            inc=1,
            device_id=((f + df) % nf, (t + dt) % nt),
            device_id_type=MESH,
        )
    x_copy.wait()
    scales = scales_ref[...].reshape(frames * rows, columns).T
    for i in range(frames):
        for j in range(rows):
            at = i * rows + j
            ext[0, frames + i, 1 + j] = (codes[i, j].astype(F32) * scales[:, at : at + 1]).astype(
                BF16
            )
    pl.semaphore_wait(barrier, len(offsets))

    def halo(e):
        step = 1 if e < layers else -1
        own = frames if step > 0 else 0
        far = 0 if step > 0 else frames
        messages = []
        for index, (df, dt) in enumerate(((step, 0), (0, 1), (0, -1), (step, 1), (step, -1))):
            if dt == 0:
                src_rows, dst_rows = (1, 1 + rows), (1, 1 + rows)
            elif dt > 0:
                src_rows, dst_rows = (rows, rows + 1), (0, 1)
            else:
                src_rows, dst_rows = (1, 2), (rows + 1, rows + 2)
            start = far if df else own
            to_f, to_t, from_f, from_t = f + df, t + dt, f - df, t - dt
            can_send = (to_f >= 0) & (to_f < nf) & (to_t >= 0) & (to_t < nt)
            can_recv = (from_f >= 0) & (from_f < nf) & (from_t >= 0) & (from_t < nt)
            copy = pltpu.make_async_remote_copy(
                src_ref=ext.at[e, own : own + frames, src_rows[0] : src_rows[1]],
                dst_ref=ext.at[e, start : start + frames, dst_rows[0] : dst_rows[1]],
                send_sem=halo_send.at[e, index],
                recv_sem=halo_recv.at[e, index],
                device_id=((f + df) % nf, (t + dt) % nt),
                device_id_type=MESH,
            )
            messages.append((copy, can_send, can_recv))
        return messages

    halos = [halo(e) for e in range(2 * layers)]

    def send_halo(e):
        for copy, can_send, _ in halos[e]:
            pl.when(can_send)(copy.start)

    def wait_halo(e, indices):
        for index in indices:
            copy, _, can_recv = halos[e][index]
            pl.when(can_recv)(copy.wait_recv)

    height = frames * (rows + 2) * columns
    column = lax.broadcasted_iota(jnp.int32, (height, channels), 0) % columns

    def fill(target, e, first):
        part = ext[e, first : first + frames].reshape(height, channels)
        flat = part.astype(F32)
        before = jnp.where(column == 0, 0.0, pltpu.roll(flat, 1, 0)).astype(BF16)
        after = jnp.where(column == columns - 1, 0.0, pltpu.roll(flat, height - 1, 0)).astype(BF16)
        low = first * block
        for c, value in enumerate((before, part, after)):
            value = value.reshape(frames, rows + 2, columns, channels)
            for b in range(3):
                at = (3 * b + c) * channels
                target[low : low + cells, at : at + channels] = value[:, b : b + rows].reshape(
                    cells, channels
                )

    def convolve(target, e, weight):
        forward = e < layers
        own, far = (frames, 0) if forward else (0, frames)

        def product(low, high, order):
            return jnp.dot(
                target[low * block : high * block, :],
                weight(order if forward else 2 - order),
                preferred_element_type=F32,
            )

        wait_halo(e, (1, 2))
        fill(target, e, own)
        if forward:
            summed[...] = product(2, 4, 2)
            summed[block:cells] += product(2, 3, 1)
        else:
            summed[...] = product(0, 2, 0)
            summed[0:block] += product(1, 2, 1)
        wait_halo(e, (0, 3, 4))
        fill(target, e, far)
        if forward:
            summed[0:block] += product(1, 2, 1)
            return summed[...] + product(0, 2, 0)
        summed[block:cells] += product(2, 3, 1)
        return summed[...] + product(2, 4, 2)

    def turn(l):
        for k in range(27):
            a, m = k // 9, 8 - k % 9
            turned[l, a, m * channels : (m + 1) * channels, :] = weights[l, k].T

    def remote(source, target, sends, recvs, device):
        return pltpu.make_async_remote_copy(
            src_ref=source,
            dst_ref=target,
            send_sem=sends,
            recv_sem=recvs,
            device_id=device,
            device_id_type=MESH,
        )

    partner = (f, t + 1 - 2 * core)

    def pair_copy(l):
        return remote(
            pair_out.at[l, 1 - core], pair_in.at[l], pair_send.at[l], pair_recv.at[l], partner
        )

    def ring_copy(l, s):
        peer = (place + s) % pairs
        return remote(
            ring_out.at[l, peer],
            ring_in.at[l, s - 1],
            ring_send.at[l, s - 1],
            ring_recv.at[l, s - 1],
            (f, 2 * peer + core),
        )

    def pack_copy(l, s):
        peer = (f + s) % nf
        return remote(
            pack_out.at[l, peer],
            pack_in.at[l, s - 1],
            pack_send.at[l, s - 1],
            pack_recv.at[l, s - 1],
            (peer, t),
        )

    def wide_pair_copy(l, d):
        return remote(
            wide_pair_out.at[l, d, 1 - core],
            wide_pair_in.at[l, d],
            wide_pair_send.at[l, d],
            wide_pair_recv.at[l, d],
            partner,
        )

    def wide_frame_copy(l, s):
        peer = (f + s) % nf
        return remote(
            wide_frame_out.at[l, peer],
            wide_frame_in.at[l, s - 1],
            wide_frame_send.at[l, s - 1],
            wide_frame_recv.at[l, s - 1],
            (peer, t),
        )

    def wide_ring_copy(l, s):
        peer = (place + s) % pairs
        return remote(
            wide_ring_out.at[l, peer],
            wide_ring_in.at[l, s - 1],
            wide_ring_send.at[l, s - 1],
            wide_ring_recv.at[l, s - 1],
            (f, 2 * peer + core),
        )

    def packed(source, size, d):
        height = source.shape[1]
        lane_block = lax.broadcasted_iota(jnp.int32, (size * height, channels), 1) // own_o
        result = jnp.zeros((size * height, channels), F32)
        for j in range(nf):
            piece = source[j * size : (j + 1) * size].reshape(size * height, channels)
            shift = ((j - d) * own_o) % channels
            if shift:
                piece = pltpu.roll(piece, shift, 1)
            result = jnp.where(lane_block == j, piece, result)
        return result.reshape(size, height, channels)

    def unpack(value, size, first, count):
        for j in range(nf):
            low, high = j * size, min(count, (j + 1) * size)
            if low >= high:
                break
            moved = value
            if j:
                moved = pltpu.roll(
                    value.reshape(size * own_q, channels), channels - j * own_o, 1
                ).reshape(size, own_q, channels)
            kg_ref[first + low : first + high] = moved[: high - low, :, :own_o]

    def kernel_term(l, a, pre_grad):
        part = lax.dot_general(
            patch[l, a * block : a * block + cells, :],
            pre_grad,
            (((0,), (0,)), ((), ())),
            preferred_element_type=F32,
        )
        return part.reshape(9, channels, channels)

    def kernel_terms(l, pre_grad):
        for a in (1, 2):
            terms[9 * a - 9 : 9 * a] = kernel_term(l, a, pre_grad)
        for d in range(nf):
            part = packed(terms, wide, d).astype(BF16)
            for q in range(nt):
                wide_pair_out[l, d, q % 2, q // 2] = part[:, q * own_q : (q + 1) * own_q]
            wide_pair_copy(l, d).start()
        part = kernel_term(l, 0, pre_grad).astype(BF16)
        for q in range(nt):
            pair_out[l, q % 2, q // 2] = part[:, q * own_q : (q + 1) * own_q]
        pair_copy(l).start()

    def ring_stage(l):
        for s in range(1, nf):
            peer = (f + s) % nf
            wide_pair_copy(l, peer).wait_recv()
            wide_frame_out[l, peer] = (
                wide_pair_out[l, peer, core].astype(F32) + wide_pair_in[l, peer].astype(F32)
            ).astype(BF16)
            wide_frame_copy(l, s).start()
        pair_copy(l).wait_recv()
        for s in range(1, pairs):
            peer = (place + s) % pairs
            ring_out[l, peer] = (
                pair_out[l, core, peer].astype(F32) + pair_in[l, peer].astype(F32)
            ).astype(BF16)
            ring_copy(l, s).start()
        total[l, 0:9] = pair_out[l, core, place].astype(F32) + pair_in[l, place].astype(F32)
        wide_pair_copy(l, f).wait_recv()
        wide_total[l] = wide_pair_out[l, f, core].astype(F32) + wide_pair_in[l, f].astype(F32)

    def pack_stage(l):
        for s in range(1, nf):
            wide_frame_copy(l, s).wait_recv()

        def wide_sum(p):
            value = wide_total[l, p]
            for s in range(1, nf):
                value = value + wide_frame_in[l, s - 1, p].astype(F32)
            return value

        for s in range(1, pairs):
            peer = (place + s) % pairs
            wide_ring_out[l, peer] = wide_sum(peer).astype(BF16)
            wide_ring_copy(l, s).start()
        wide_total[l, place] = wide_sum(place)
        value = total[l, 0:9]
        for s in range(1, pairs):
            ring_copy(l, s).wait_recv()
            value = value + ring_in[l, s - 1].astype(F32)
        total[l, 0:9] = value
        for d in range(nf):
            pack_out[l, d] = packed(total.at[l], group, d).astype(BF16)
        for s in range(1, nf):
            pack_copy(l, s).start()

    def finish(l):
        value = wide_total[l, place]
        for s in range(1, pairs):
            wide_ring_copy(l, s).wait_recv()
            value = value + wide_ring_in[l, s - 1].astype(F32)
        unpack(value * scale, wide, 27 * l + 9, 18)
        value = pack_out[l, f].astype(F32)
        for s in range(1, nf):
            pack_copy(l, s).wait_recv()
            value = value + pack_in[l, s - 1].astype(F32)
        unpack(value * scale, group, 27 * l, 9)

    scale = 1.0 / math.sqrt(cells * nf * nt)
    send_halo(0)
    for l in range(layers):
        if nf * group > 9:
            total[l, 9:] = jnp.zeros((nf * group - 9, own_q, channels), F32)
    if nf * wide > 18:
        terms[18:] = jnp.zeros((nf * wide - 18, channels, channels), F32)
    for l in range(layers):
        w_copies[l].wait()
        if l == 0:
            turn(layers - 1 if layers == 1 else 0)
        else:
            turn(l)
        z = convolve(
            patch.at[l],
            l,
            lambda a: weights[l, 9 * a : 9 * a + 9].reshape(9 * channels, channels),
        )
        z_keep[l] = z
        if l + 1 < layers:
            inverse = lax.rsqrt(jnp.mean(z * z, axis=-1, keepdims=True) + EPS)
            normed = z * inverse * gains_ref[l : l + 1, :]
            ext[l + 1, frames : 2 * frames, 1 : 1 + rows] = (
                (normed * sigmoid(normed)).astype(BF16).reshape(frames, rows, columns, channels)
            )
            send_halo(l + 1)

    cot_copy.wait()
    upstream = cot[...].astype(F32).reshape(cells, channels)
    for l in reversed(range(layers)):
        e = layers + l
        z = z_keep[l]
        gain = gains_ref[l : l + 1, :]
        inverse = lax.rsqrt(jnp.mean(z * z, axis=-1, keepdims=True) + EPS)
        normed = z * inverse * gain
        sigma = sigmoid(normed)
        scaled = gain * upstream * sigma * (1.0 + normed * (1.0 - sigma))
        mixed = jnp.mean(z * scaled, axis=-1, keepdims=True)
        pre_grad = (inverse * scaled - z * (inverse * inverse * inverse * mixed)).astype(BF16)
        ext[e, 0:frames, 1 : 1 + rows] = pre_grad.reshape(frames, rows, columns, channels)
        send_halo(e)
        kernel_terms(l, pre_grad)
        if l + 1 < layers:
            pack_stage(l + 1)
        ring_stage(l)
        back = convolve(patch_back, e, lambda a: turned[l, a])
        back = back.astype(BF16)
        upstream = back.astype(F32)
        if l + 1 < layers:
            finish(l + 1)
    grad_ref[...] = back.reshape(frames, rows, columns, channels)
    pack_stage(0)
    finish(0)

    for e in range(2 * layers):
        for copy, can_send, _ in halos[e]:
            pl.when(can_send)(copy.wait_send)
    for l in range(layers):
        pair_copy(l).wait_send()
        for d in range(nf):
            wide_pair_copy(l, d).wait_send()
        for s in range(1, pairs):
            ring_copy(l, s).wait_send()
            wide_ring_copy(l, s).wait_send()
        for s in range(1, nf):
            pack_copy(l, s).wait_send()
            wide_frame_copy(l, s).wait_send()


def local(saved_codes, saved_scales, kernels, norm_gains, cotangent):
    nf, nt = lax.axis_size("frame"), lax.axis_size("tile")
    frames, rows, columns, channels = saved_codes.shape
    layers = kernels.shape[0]
    assert frames == 2
    block = rows * columns
    cells = frames * block
    pairs = nt // 2
    own_q, own_o = channels // nt, channels // nf
    group, wide = -(-9 // nf), -(-18 // nf)
    vmem = pl.BlockSpec(memory_space=pltpu.VMEM)
    hbm = pl.BlockSpec(memory_space=pltpu.HBM)
    dma = pltpu.SemaphoreType.DMA
    input_grad, summed = pl.pallas_call(
        functools.partial(kernel, (nf, nt, layers, frames, rows, columns, channels)),
        out_shape=(
            jax.ShapeDtypeStruct((frames, rows, columns, channels), BF16),
            jax.ShapeDtypeStruct((27 * layers, own_q, own_o), F32),
        ),
        in_specs=[hbm, vmem, hbm, vmem, hbm],
        out_specs=(vmem, vmem),
        scratch_shapes=[
            pltpu.VMEM((2 * layers, 2 * frames, rows + 2, columns, channels), BF16),
            pltpu.VMEM((layers, 27, channels, channels), BF16),
            pltpu.VMEM((layers, 3, 9 * channels, channels), BF16),
            pltpu.VMEM((frames, rows, columns, channels), BF16),
            pltpu.VMEM((frames, rows, columns, channels), BF16),
            pltpu.VMEM((layers, 2 * cells, 9 * channels), BF16),
            pltpu.VMEM((2 * cells, 9 * channels), BF16),
            pltpu.VMEM((layers, cells, channels), F32),
            pltpu.VMEM((cells, channels), F32),
            pltpu.VMEM((nf * wide, channels, channels), F32),
            pltpu.VMEM((layers, 2, pairs, 9, own_q, channels), BF16),
            pltpu.VMEM((layers, pairs, 9, own_q, channels), BF16),
            pltpu.VMEM((layers, pairs, 9, own_q, channels), BF16),
            pltpu.VMEM((layers, pairs - 1, 9, own_q, channels), BF16),
            pltpu.VMEM((layers, nf * group, own_q, channels), F32),
            pltpu.VMEM((layers, nf, group, own_q, channels), BF16),
            pltpu.VMEM((layers, nf - 1, group, own_q, channels), BF16),
            pltpu.VMEM((layers, nf, 2, pairs, wide, own_q, channels), BF16),
            pltpu.VMEM((layers, nf, pairs, wide, own_q, channels), BF16),
            pltpu.VMEM((layers, nf, pairs, wide, own_q, channels), BF16),
            pltpu.VMEM((layers, nf - 1, pairs, wide, own_q, channels), BF16),
            pltpu.VMEM((layers, pairs, wide, own_q, channels), F32),
            pltpu.VMEM((layers, pairs, wide, own_q, channels), BF16),
            pltpu.VMEM((layers, pairs - 1, wide, own_q, channels), BF16),
            dma((2 + layers,)),
            dma((2 * layers, 5)),
            dma((2 * layers, 5)),
            dma((layers,)),
            dma((layers,)),
            dma((layers, pairs - 1)),
            dma((layers, pairs - 1)),
            dma((layers, nf - 1)),
            dma((layers, nf - 1)),
            dma((layers, nf)),
            dma((layers, nf)),
            dma((layers, nf - 1)),
            dma((layers, nf - 1)),
            dma((layers, pairs - 1)),
            dma((layers, pairs - 1)),
        ],
        compiler_params=pltpu.CompilerParams(
            collective_id=0, has_side_effects=True, vmem_limit_bytes=65_700_000
        ),
    )(saved_codes, saved_scales, kernels, norm_gains, cotangent)
    return input_grad, summed


def solution(mesh):
    in_specs = (
        P("frame", "tile", None, None),
        P("frame", "tile", None),
        P(),
        P(),
        P("frame", "tile", None, None),
    )
    out_specs = (P("frame", "tile", None, None), P(None, "tile", "frame"))
    return jax.shard_map(local, mesh=mesh, in_specs=in_specs, out_specs=out_specs, check_vma=False)
```

```python
import functools
import math

import jax
import jax.numpy as jnp
from jax import lax
from jax.experimental import pallas as pl
from jax.experimental.pallas import tpu as pltpu
from jax.sharding import PartitionSpec as P

EPS = 1e-06
MESH = pl.DeviceIdType.MESH
F32 = jnp.float32
BF16 = jnp.bfloat16


def sigmoid(value):
    return 1.0 / (1.0 + jnp.exp(-value))


def kernel(
    sizes,
    codes_in,
    scales_ref,
    w_in,
    gains_ref,
    cot_in,
    grad_ref,
    kg_ref,
    ext,
    weights,
    turned,
    cot,
    codes,
    patch,
    patch_back,
    z_keep,
    summed,
    terms,
    pair_out,
    pair_in,
    ring_out,
    ring_in,
    total,
    pack_out,
    pack_in,
    wide_pair_out,
    wide_pair_in,
    wide_frame_out,
    wide_frame_in,
    wide_total,
    wide_ring_out,
    wide_ring_in,
    local_sem,
    halo_send,
    halo_recv,
    pair_send,
    pair_recv,
    ring_send,
    ring_recv,
    pack_send,
    pack_recv,
    wide_pair_send,
    wide_pair_recv,
    wide_frame_send,
    wide_frame_recv,
    wide_ring_send,
    wide_ring_recv,
):
    nf, nt, layers, frames, rows, columns, channels = sizes
    f = lax.axis_index("frame")
    t = lax.axis_index("tile")
    pairs = nt // 2
    core = t % 2
    place = t // 2
    block = rows * columns
    cells = frames * block
    own_q = channels // nt
    own_o = channels // nf
    group, wide = -(-9 // nf), -(-18 // nf)

    x_copy = pltpu.make_async_copy(codes_in, codes, local_sem.at[0])
    w_copies = [
        pltpu.make_async_copy(w_in.at[l], weights.at[l], local_sem.at[1 + l]) for l in range(layers)
    ]
    cot_copy = pltpu.make_async_copy(cot_in, cot, local_sem.at[1 + layers])
    x_copy.start()
    for c in w_copies:
        c.start()
    cot_copy.start()
    for e in range(2 * layers):
        edge = jnp.zeros((2 * frames, 1, columns, channels), BF16)
        ext[e, :, 0:1] = edge
        ext[e, :, rows + 1 : rows + 2] = edge
        far = 0 if e < layers else frames
        ext[e, far : far + frames, 1 : 1 + rows] = jnp.zeros(
            (frames, rows, columns, channels), BF16
        )

    offsets = {(0, 1), (0, nt - 1)}
    for df in (1, nf - 1):
        for dt in (0, 1, nt - 1):
            offsets.add((df, dt))
    for s in range(1, pairs):
        offsets.add((0, 2 * s))
    for s in range(1, nf):
        offsets.add((s, 0))
    offsets = sorted(offsets)
    barrier = pltpu.get_barrier_semaphore()
    for df, dt in offsets:
        pl.semaphore_signal(
            barrier,
            inc=1,
            device_id=((f + df) % nf, (t + dt) % nt),
            device_id_type=MESH,
        )
    x_copy.wait()
    scales = scales_ref[...].reshape(frames * rows, columns).T
    for i in range(frames):
        for j in range(rows):
            at = i * rows + j
            ext[0, frames + i, 1 + j] = (codes[i, j].astype(F32) * scales[:, at : at + 1]).astype(
                BF16
            )
    pl.semaphore_wait(barrier, len(offsets))

    def halo(e):
        step = 1 if e < layers else -1
        own = frames if step > 0 else 0
        far = 0 if step > 0 else frames
        messages = []
        for index, (df, dt) in enumerate(((step, 0), (0, 1), (0, -1), (step, 1), (step, -1))):
            if dt == 0:
                src_rows, dst_rows = (1, 1 + rows), (1, 1 + rows)
            elif dt > 0:
                src_rows, dst_rows = (rows, rows + 1), (0, 1)
            else:
                src_rows, dst_rows = (1, 2), (rows + 1, rows + 2)
            start = far if df else own
            to_f, to_t, from_f, from_t = f + df, t + dt, f - df, t - dt
            can_send = (to_f >= 0) & (to_f < nf) & (to_t >= 0) & (to_t < nt)
            can_recv = (from_f >= 0) & (from_f < nf) & (from_t >= 0) & (from_t < nt)
            copy = pltpu.make_async_remote_copy(
                src_ref=ext.at[e, own : own + frames, src_rows[0] : src_rows[1]],
                dst_ref=ext.at[e, start : start + frames, dst_rows[0] : dst_rows[1]],
                send_sem=halo_send.at[e, index],
                recv_sem=halo_recv.at[e, index],
                device_id=((f + df) % nf, (t + dt) % nt),
                device_id_type=MESH,
            )
            messages.append((copy, can_send, can_recv))
        return messages

    halos = [halo(e) for e in range(2 * layers)]

    def send_halo(e):
        for copy, can_send, _ in halos[e]:
            pl.when(can_send)(copy.start)

    def wait_halo(e, indices):
        for index in indices:
            copy, _, can_recv = halos[e][index]
            pl.when(can_recv)(copy.wait_recv)

    height = frames * (rows + 2) * columns
    column = lax.broadcasted_iota(jnp.int32, (height, channels), 0) % columns

    def fill(target, e, first):
        part = ext[e, first : first + frames].reshape(height, channels)
        flat = part.astype(F32)
        before = jnp.where(column == 0, 0.0, pltpu.roll(flat, 1, 0)).astype(BF16)
        after = jnp.where(column == columns - 1, 0.0, pltpu.roll(flat, height - 1, 0)).astype(BF16)
        low = first * block
        for c, value in enumerate((before, part, after)):
            value = value.reshape(frames, rows + 2, columns, channels)
            for b in range(3):
                at = (3 * b + c) * channels
                target[low : low + cells, at : at + channels] = value[:, b : b + rows].reshape(
                    cells, channels
                )

    def convolve(target, e, weight):
        forward = e < layers
        own, far = (frames, 0) if forward else (0, frames)

        def product(low, high, order):
            return jnp.dot(
                target[low * block : high * block, :],
                weight(order if forward else 2 - order),
                preferred_element_type=F32,
            )

        wait_halo(e, (1, 2))
        fill(target, e, own)
        if forward:
            summed[...] = product(2, 4, 2)
            summed[block:cells] += product(2, 3, 1)
        else:
            summed[...] = product(0, 2, 0)
            summed[0:block] += product(1, 2, 1)
        wait_halo(e, (0, 3, 4))
        fill(target, e, far)
        if forward:
            summed[0:block] += product(1, 2, 1)
            return summed[...] + product(0, 2, 0)
        summed[block:cells] += product(2, 3, 1)
        return summed[...] + product(2, 4, 2)

    def turn(l):
        for k in range(27):
            a, m = k // 9, 8 - k % 9
            turned[l, a, m * channels : (m + 1) * channels, :] = weights[l, k].T

    def remote(source, target, sends, recvs, device):
        return pltpu.make_async_remote_copy(
            src_ref=source,
            dst_ref=target,
            send_sem=sends,
            recv_sem=recvs,
            device_id=device,
            device_id_type=MESH,
        )

    partner = (f, t + 1 - 2 * core)

    def pair_copy(l):
        return remote(
            pair_out.at[l, 1 - core], pair_in.at[l], pair_send.at[l], pair_recv.at[l], partner
        )

    def ring_copy(l, s):
        peer = (place + s) % pairs
        return remote(
            ring_out.at[l, peer],
            ring_in.at[l, s - 1],
            ring_send.at[l, s - 1],
            ring_recv.at[l, s - 1],
            (f, 2 * peer + core),
        )

    def pack_copy(l, s):
        peer = (f + s) % nf
        return remote(
            pack_out.at[l, peer],
            pack_in.at[l, s - 1],
            pack_send.at[l, s - 1],
            pack_recv.at[l, s - 1],
            (peer, t),
        )

    def wide_pair_copy(l, d):
        return remote(
            wide_pair_out.at[l, d, 1 - core],
            wide_pair_in.at[l, d],
            wide_pair_send.at[l, d],
            wide_pair_recv.at[l, d],
            partner,
        )

    def wide_frame_copy(l, s):
        peer = (f + s) % nf
        return remote(
            wide_frame_out.at[l, peer],
            wide_frame_in.at[l, s - 1],
            wide_frame_send.at[l, s - 1],
            wide_frame_recv.at[l, s - 1],
            (peer, t),
        )

    def wide_ring_copy(l, s):
        peer = (place + s) % pairs
        return remote(
            wide_ring_out.at[l, peer],
            wide_ring_in.at[l, s - 1],
            wide_ring_send.at[l, s - 1],
            wide_ring_recv.at[l, s - 1],
            (f, 2 * peer + core),
        )

    def packed(source, size, d):
        height = source.shape[1]
        lane_block = lax.broadcasted_iota(jnp.int32, (size * height, channels), 1) // own_o
        result = jnp.zeros((size * height, channels), F32)
        for j in range(nf):
            piece = source[j * size : (j + 1) * size].reshape(size * height, channels)
            shift = ((j - d) * own_o) % channels
            if shift:
                piece = pltpu.roll(piece, shift, 1)
            result = jnp.where(lane_block == j, piece, result)
        return result.reshape(size, height, channels)

    def unpack(value, size, first, count):
        for j in range(nf):
            low, high = j * size, min(count, (j + 1) * size)
            if low >= high:
                break
            moved = value
            if j:
                moved = pltpu.roll(
                    value.reshape(size * own_q, channels), channels - j * own_o, 1
                ).reshape(size, own_q, channels)
            kg_ref[first + low : first + high] = moved[: high - low, :, :own_o]

    def kernel_term(l, a, pre_grad):
        part = lax.dot_general(
            patch[l, a * block : a * block + cells, :],
            pre_grad,
            (((0,), (0,)), ((), ())),
            preferred_element_type=F32,
        )
        return part.reshape(9, channels, channels)

    def kernel_terms(l, pre_grad):
        for a in (1, 2):
            terms[9 * a - 9 : 9 * a] = kernel_term(l, a, pre_grad)
        for d in range(nf):
            part = packed(terms, wide, d).astype(BF16)
            for q in range(nt):
                wide_pair_out[l, d, q % 2, q // 2] = part[:, q * own_q : (q + 1) * own_q]
            wide_pair_copy(l, d).start()
        part = kernel_term(l, 0, pre_grad).astype(BF16)
        for q in range(nt):
            pair_out[l, q % 2, q // 2] = part[:, q * own_q : (q + 1) * own_q]
        pair_copy(l).start()

    def ring_stage(l):
        for s in range(1, nf):
            peer = (f + s) % nf
            wide_pair_copy(l, peer).wait_recv()
            wide_frame_out[l, peer] = (
                wide_pair_out[l, peer, core].astype(F32) + wide_pair_in[l, peer].astype(F32)
            ).astype(BF16)
            wide_frame_copy(l, s).start()
        pair_copy(l).wait_recv()
        for s in range(1, pairs):
            peer = (place + s) % pairs
            ring_out[l, peer] = (
                pair_out[l, core, peer].astype(F32) + pair_in[l, peer].astype(F32)
            ).astype(BF16)
            ring_copy(l, s).start()
        total[l, 0:9] = pair_out[l, core, place].astype(F32) + pair_in[l, place].astype(F32)
        wide_pair_copy(l, f).wait_recv()
        wide_total[l] = wide_pair_out[l, f, core].astype(F32) + wide_pair_in[l, f].astype(F32)

    def pack_stage(l):
        for s in range(1, nf):
            wide_frame_copy(l, s).wait_recv()

        def wide_sum(p):
            value = wide_total[l, p]
            for s in range(1, nf):
                value = value + wide_frame_in[l, s - 1, p].astype(F32)
            return value

        for s in range(1, pairs):
            peer = (place + s) % pairs
            wide_ring_out[l, peer] = wide_sum(peer).astype(BF16)
            wide_ring_copy(l, s).start()
        wide_total[l, place] = wide_sum(place)
        value = total[l, 0:9]
        for s in range(1, pairs):
            ring_copy(l, s).wait_recv()
            value = value + ring_in[l, s - 1].astype(F32)
        total[l, 0:9] = value
        for d in range(nf):
            pack_out[l, d] = packed(total.at[l], group, d).astype(BF16)
        for s in range(1, nf):
            pack_copy(l, s).start()

    def finish(l):
        value = wide_total[l, place]
        for s in range(1, pairs):
            wide_ring_copy(l, s).wait_recv()
            value = value + wide_ring_in[l, s - 1].astype(F32)
        unpack(value * scale, wide, 27 * l + 9, 18)
        value = pack_out[l, f].astype(F32)
        for s in range(1, nf):
            pack_copy(l, s).wait_recv()
            value = value + pack_in[l, s - 1].astype(F32)
        unpack(value * scale, group, 27 * l, 9)

    scale = 1.0 / math.sqrt(cells * nf * nt)
    send_halo(0)
    for l in range(layers):
        if nf * group > 9:
            total[l, 9:] = jnp.zeros((nf * group - 9, own_q, channels), F32)
    if nf * wide > 18:
        terms[18:] = jnp.zeros((nf * wide - 18, channels, channels), F32)
    for l in range(layers):
        w_copies[l].wait()
        if l == 0:
            turn(layers - 1 if layers == 1 else 0)
        else:
            turn(l)
        z = convolve(
            patch.at[l],
            l,
            lambda a: weights[l, 9 * a : 9 * a + 9].reshape(9 * channels, channels),
        )
        z_keep[l] = z
        if l + 1 < layers:
            inverse = lax.rsqrt(jnp.mean(z * z, axis=-1, keepdims=True) + EPS)
            normed = z * inverse * gains_ref[l : l + 1, :]
            ext[l + 1, frames : 2 * frames, 1 : 1 + rows] = (
                (normed * sigmoid(normed)).astype(BF16).reshape(frames, rows, columns, channels)
            )
            send_halo(l + 1)

    cot_copy.wait()
    upstream = cot[...].astype(F32).reshape(cells, channels)
    for l in reversed(range(layers)):
        e = layers + l
        z = z_keep[l]
        gain = gains_ref[l : l + 1, :]
        inverse = lax.rsqrt(jnp.mean(z * z, axis=-1, keepdims=True) + EPS)
        normed = z * inverse * gain
        sigma = sigmoid(normed)
        scaled = gain * upstream * sigma * (1.0 + normed * (1.0 - sigma))
        mixed = jnp.mean(z * scaled, axis=-1, keepdims=True)
        pre_grad = (inverse * scaled - z * (inverse * inverse * inverse * mixed)).astype(BF16)
        ext[e, 0:frames, 1 : 1 + rows] = pre_grad.reshape(frames, rows, columns, channels)
        send_halo(e)
        kernel_terms(l, pre_grad)
        if l + 1 < layers:
            pack_stage(l + 1)
        ring_stage(l)
        back = convolve(patch_back, e, lambda a: turned[l, a])
        back = back.astype(BF16)
        upstream = back.astype(F32)
        if l + 1 < layers:
            finish(l + 1)
    grad_ref[...] = back.reshape(frames, rows, columns, channels)
    pack_stage(0)
    finish(0)

    for e in range(2 * layers):
        for copy, can_send, _ in halos[e]:
            pl.when(can_send)(copy.wait_send)
    for l in range(layers):
        pair_copy(l).wait_send()
        for d in range(nf):
            wide_pair_copy(l, d).wait_send()
        for s in range(1, pairs):
            ring_copy(l, s).wait_send()
            wide_ring_copy(l, s).wait_send()
        for s in range(1, nf):
            pack_copy(l, s).wait_send()
            wide_frame_copy(l, s).wait_send()


def local(saved_codes, saved_scales, kernels, norm_gains, cotangent):
    nf, nt = lax.axis_size("frame"), lax.axis_size("tile")
    frames, rows, columns, channels = saved_codes.shape
    layers = kernels.shape[0]
    assert frames == 2
    block = rows * columns
    cells = frames * block
    pairs = nt // 2
    own_q, own_o = channels // nt, channels // nf
    group, wide = -(-9 // nf), -(-18 // nf)
    vmem = pl.BlockSpec(memory_space=pltpu.VMEM)
    hbm = pl.BlockSpec(memory_space=pltpu.HBM)
    dma = pltpu.SemaphoreType.DMA
    input_grad, summed = pl.pallas_call(
        functools.partial(kernel, (nf, nt, layers, frames, rows, columns, channels)),
        out_shape=(
            pltpu.VMEM((frames, rows, columns, channels), BF16),
            pltpu.VMEM((27 * layers, own_q, own_o), F32),
        ),
        in_specs=[hbm, vmem, hbm, vmem, hbm],
        out_specs=(vmem, vmem),
        scratch_shapes=[
            pltpu.VMEM((2 * layers, 2 * frames, rows + 2, columns, channels), BF16),
            pltpu.VMEM((layers, 27, channels, channels), BF16),
            pltpu.VMEM((layers, 3, 9 * channels, channels), BF16),
            pltpu.VMEM((frames, rows, columns, channels), BF16),
            pltpu.VMEM((frames, rows, columns, channels), BF16),
            pltpu.VMEM((layers, 2 * cells, 9 * channels), BF16),
            pltpu.VMEM((2 * cells, 9 * channels), BF16),
            pltpu.VMEM((layers, cells, channels), F32),
            pltpu.VMEM((cells, channels), F32),
            pltpu.VMEM((nf * wide, channels, channels), F32),
            pltpu.VMEM((layers, 2, pairs, 9, own_q, channels), BF16),
            pltpu.VMEM((layers, pairs, 9, own_q, channels), BF16),
            pltpu.VMEM((layers, pairs, 9, own_q, channels), BF16),
            pltpu.VMEM((layers, pairs - 1, 9, own_q, channels), BF16),
            pltpu.VMEM((layers, nf * group, own_q, channels), F32),
            pltpu.VMEM((layers, nf, group, own_q, channels), BF16),
            pltpu.VMEM((layers, nf - 1, group, own_q, channels), BF16),
            pltpu.VMEM((layers, nf, 2, pairs, wide, own_q, channels), BF16),
            pltpu.VMEM((layers, nf, pairs, wide, own_q, channels), BF16),
            pltpu.VMEM((layers, nf, pairs, wide, own_q, channels), BF16),
            pltpu.VMEM((layers, nf - 1, pairs, wide, own_q, channels), BF16),
            pltpu.VMEM((layers, pairs, wide, own_q, channels), F32),
            pltpu.VMEM((layers, pairs, wide, own_q, channels), BF16),
            pltpu.VMEM((layers, pairs - 1, wide, own_q, channels), BF16),
            dma((2 + layers,)),
            dma((2 * layers, 5)),
            dma((2 * layers, 5)),
            dma((layers,)),
            dma((layers,)),
            dma((layers, pairs - 1)),
            dma((layers, pairs - 1)),
            dma((layers, nf - 1)),
            dma((layers, nf - 1)),
            dma((layers, nf)),
            dma((layers, nf)),
            dma((layers, nf - 1)),
            dma((layers, nf - 1)),
            dma((layers, pairs - 1)),
            dma((layers, pairs - 1)),
        ],
        compiler_params=pltpu.CompilerParams(
            collective_id=0, has_side_effects=True, vmem_limit_bytes=62_000_000
        ),
    )(saved_codes, saved_scales, kernels, norm_gains, cotangent)
    return input_grad, summed


def solution(mesh):
    in_specs = (
        P("frame", "tile", None, None),
        P("frame", "tile", None),
        P(),
        P(),
        P("frame", "tile", None, None),
    )
    out_specs = (P("frame", "tile", None, None), P(None, "tile", "frame"))
    return jax.shard_map(local, mesh=mesh, in_specs=in_specs, out_specs=out_specs, check_vma=False)
```
